512 devices in a mesh: segment: 8 (over x, core), dp: 64 (over y, z).
Axes of the slice: x: 4, y: 4, z: 16, core: 2. Of those that a mesh axis runs over, the one named last changes fastest.
Arguments:
- hidden: bfloat16 [8, 8192, 8192], P('segment', 'dp'), may hold values from -6 to 6
- store_a: bfloat16 [8, 32, 64, 8192], P('segment', None, None, 'dp'), may hold values from -0.0625 to 0.0625
- store_b: bfloat16 [8, 32, 64, 8192], P('segment', None, None, 'dp'), may hold values from -0.75 to 0.75
- request_start: int32 [8, 32], P('segment'), may hold values from 0 to 8128, as said below
- request_adapter: int32 [8, 32], P('segment'), may hold values from 0 to 31
Outputs:
- updated: bfloat16 [8, 8192, 8192], P('segment', 'dp')
The draws below stay inside these ranges and needn't reach their ends.
Inputs may be any that keep to these rules, and one draw needn't show every extreme that they name: `request_start`: in each group the starts rise strictly from 0, are multiples of 64, and the last is 8128.
All inputs are finite; a program needn't handle non-finite values.
Results may differ from the reference program's by a relative error of at most 0.006.
Values may be sent and summed in bfloat16 or wider, within the bound.
No kernel may reach another device: no remote copies, remote signals or barrier semaphores. Data moves between devices by JAX's collectives and lax.ppermute only.
A program may use at most 64 MiB of HBM per device.

```python
import math
import jax
import jax.numpy as jnp
import numpy as np
from jax import lax

MODEL_WIDTH = 8192
R = 64
ADAPTERS = 32
BLOCK = 64
STEPS = 2
SEGMENTS = 8
GROUP_TOKENS = 8192
REQUESTS = 32


def draw_request_start(key, part):
    blocks = GROUP_TOKENS // BLOCK

    def single_group(group_key):
        inner = jax.random.permutation(group_key, blocks - 2) + 1
        picked = jnp.sort(inner[:REQUESTS - 2]).astype(jnp.int32)
        first = jnp.zeros((1,), jnp.int32)
        final = jnp.full((1,), blocks - 1, jnp.int32)
        return jnp.concatenate([first, picked, final]) * BLOCK
    return jax.vmap(single_group)(jax.random.split(key, SEGMENTS)).astype(jnp.int32)


def with_ends(entries, stream_key, smallest, largest):
    longest = entries.shape.index(max(entries.shape))
    spots = []
    for shift in (0, 1):
        where = [jax.random.randint(jax.random.fold_in(stream_key, axis), (), 0, length) for axis, length in enumerate(entries.shape)]
        where[longest] = (where[longest] + shift) % entries.shape[longest]
        spots.append(tuple(where))
    return entries.at[spots[0]].set(smallest).at[spots[1]].set(largest)


def shard_levels(stream_key, shape, cuts, smallest, top_value):
    def one(position, blocks):
        draws = jax.random.uniform(jax.random.fold_in(jax.random.fold_in(stream_key, 6), position), (blocks,), jnp.float32, smallest / len(cuts), top_value / len(cuts))
        return jnp.repeat(jnp.exp(draws), shape[position] // blocks).reshape((-1,) + (1,) * (len(shape) - position - 1))

    gain = one(*cuts[0])
    for cut in cuts[1:]:
        gain = gain * one(*cut)
    return gain


def rank_table(amount, slope):
    loads = [(1 << 20) // math.isqrt(standing ** slope) + 1 for standing in range(1, amount + 1)]
    scale = 1 + sum(loads) // (1 << 30)
    return np.cumsum(np.array([max(1, weight // scale) for weight in loads]))


def ranked_ids(rng, dims, amount, slope):
    listing = rank_table(amount, slope)
    pick = jax.random.randint(jax.random.fold_in(rng, 1), dims, 0, int(listing[amount - 1]))
    rank = jnp.searchsorted(jnp.asarray(listing, jnp.int32), pick, side="right")
    return jax.random.permutation(jax.random.fold_in(rng, 2), amount)[rank].astype(jnp.int32)


def bell_draw(stream_key, shape, deviation, limit, cuts=(), kind=jnp.bfloat16):
    gain = shard_levels(stream_key, shape, cuts, -0.22, 0.18) if cuts else 1.0
    result = jax.random.normal(stream_key, shape, jnp.float32) * deviation * gain
    return jnp.minimum(jnp.maximum(result, -limit), limit).astype(kind)


def setup_inputs(seed: int = 0) -> dict:
    streams_of = jax.random.split(jax.random.key(seed), 6)
    return {
        "hidden": bell_draw(streams_of[0], (SEGMENTS, GROUP_TOKENS, MODEL_WIDTH), 1.0, 6.0, ((0, 8), (1, 64))),
        "store_a": bell_draw(streams_of[1], (SEGMENTS, ADAPTERS, R, MODEL_WIDTH), MODEL_WIDTH ** -0.5, 0.0625, ((0, 8), (3, 64))),
        "store_b": bell_draw(streams_of[2], (SEGMENTS, ADAPTERS, R, MODEL_WIDTH), R ** -0.5, 0.75, ((0, 8), (3, 64))),
        "request_start": draw_request_start(jax.random.fold_in(streams_of[5], 71), 0),
        "request_adapter": with_ends(ranked_ids(streams_of[4], (SEGMENTS, REQUESTS), ADAPTERS, 2), jax.random.fold_in(streams_of[4], 3), 0, ADAPTERS - 1).astype(jnp.int32),
    }


EPS = 1e-05
ADAPTER_SCALE = 0.5

def apply_layer(state, starts, adapters, panel_a, second_panel):
    value_rows = state.astype(jnp.float32)
    meansq = lax.optimization_barrier(jnp.mean(value_rows * value_rows, axis=-1, keepdims=True))
    normed = (value_rows * lax.rsqrt(meansq + EPS)).astype(jnp.bfloat16)
    blocks = GROUP_TOKENS // BLOCK
    block_start = jnp.arange(blocks, dtype=jnp.int32) * BLOCK
    request = lax.optimization_barrier(jnp.sum((starts[None, :] <= block_start[:, None]).astype(jnp.int32), axis=1)) - 1
    chosen = lax.optimization_barrier(jnp.sum(jnp.where(request[:, None] == jnp.arange(REQUESTS, dtype=jnp.int32)[None, :], adapters[None, :], 0), axis=1)).astype(jnp.int32)
    grouped = normed.reshape(blocks, BLOCK, MODEL_WIDTH).astype(jnp.float32)
    down = jnp.take(panel_a, chosen, axis=0).astype(jnp.float32)
    rank = jnp.einsum('bid,brd->bir', grouped, down).astype(jnp.bfloat16)
    upper = jnp.take(second_panel, chosen, axis=0).astype(jnp.float32)
    adapter_update = jnp.einsum('bir,brd->bid', rank.astype(jnp.float32), upper).astype(jnp.bfloat16)
    return (value_rows + ADAPTER_SCALE * adapter_update.reshape(GROUP_TOKENS, MODEL_WIDTH).astype(jnp.float32)).astype(jnp.bfloat16)

def reference(hidden, store_a, store_b, request_start, request_adapter):
    results = []
    for group in range(SEGMENTS):
        state = hidden[group]
        for step in range(STEPS):
            layer = (group + step) % SEGMENTS
            state = apply_layer(state, request_start[group], request_adapter[group], store_a[layer], store_b[layer])
        results.append(state)
    return jnp.stack(results)
```

```python
import functools

import jax
import jax.numpy as jnp
from jax import lax
from jax.experimental import pallas as pl
from jax.experimental.pallas import tpu as pltpu
from jax.sharding import Mesh, PartitionSpec as P

BLOCK = 64
EPS = 1e-05
ADAPTER_SCALE = 0.5
X, CORES, Y, Z = 4, 2, 4, 16
SEGMENT = ("x", "core")
LANES = 128
ROWS = 128
WIDTH = 8192
RANK = 64

BATCHES = (
    tuple((s, d) for d in (0, 1, 15) for s in (0, 1)),
    tuple((s, d) for d in (2, 14, 3, 13) for s in (0, 1)),
    tuple((s, d) for d in (4, 12, 5, 11) for s in (0, 1)),
    tuple((s, d) for d in (6, 10, 7, 9) for s in (0, 1)),
    tuple((s, 8) for s in (0, 1)),
)
PLACE = {
    (store, d): (b, c)
    for b, batch in enumerate(BATCHES)
    for c, (store, d) in enumerate(batch)
}
ORDER = tuple(d for batch in BATCHES for s, d in batch if s == 0)


def block_adapters(starts, adapters, total_rows):
    blocks = total_rows // BLOCK
    block_start = jnp.arange(blocks, dtype=jnp.int32) * BLOCK
    request = jnp.sum((starts[None, :] <= block_start[:, None]).astype(jnp.int32), axis=1) - 1
    labels = jnp.arange(adapters.shape[0], dtype=jnp.int32)
    picked = jnp.where(request[:, None] == labels[None, :], adapters[None, :], 0)
    return jnp.sum(picked, axis=1)


def pick_kernel(count, wanted, *refs):
    out = refs[count]
    for y in range(Y):
        for k in range(2):
            for b in range(2):
                which = wanted[y, k, b]
                for c in range(count):
                    out[y, k, c, b] = refs[c][which]


def pick(wanted, chunks):
    count = len(chunks)
    return pl.pallas_call(
        functools.partial(pick_kernel, count),
        out_shape=jax.ShapeDtypeStruct((Y, 2, count, 2, RANK, LANES), jnp.bfloat16),
        in_specs=[pl.BlockSpec(memory_space=pltpu.SMEM)]
        + [pl.BlockSpec(memory_space=pltpu.VMEM)] * count,
        out_specs=pl.BlockSpec(memory_space=pltpu.VMEM),
        compiler_params=pltpu.CompilerParams(vmem_limit_bytes=16 << 20),
        cost_estimate=pl.CostEstimate(
            flops=0, transcendentals=0, bytes_accessed=count * (3 << 18)
        ),
    )(wanted, *chunks)


def layers_kernel(z_ref, hidden, *refs):
    n = len(BATCHES)
    first, second = refs[:n], refs[n : 2 * n]
    out, state = refs[2 * n], refs[2 * n + 1]
    z = z_ref[0]

    def place(y, d):
        return pl.ds(pl.multiple_of(y * Z * LANES + ((z - d) & (Z - 1)) * LANES, LANES), LANES)

    def panel(step, store, y, d):
        b, c = PLACE[store, d]
        if step == 0:
            return first[b][y, 0, c].reshape(2 * RANK, LANES)
        return second[b][y, c].reshape(2 * RANK, LANES)

    def panels(step, store, y, ds):
        return jnp.concatenate([panel(step, store, y, d) for d in ds], axis=1)

    own = lax.broadcasted_iota(jnp.int32, (ROWS, 2 * RANK), 0) // BLOCK == (
        lax.broadcasted_iota(jnp.int32, (ROWS, 2 * RANK), 1) // RANK
    )
    groups = [(y, i, ORDER[i : i + 4]) for y in range(Y) for i in range(0, Z, 4)]

    def slot(y, i, width):
        return pl.ds((y * Z + i) * LANES, width * LANES)

    for y, i, ds in groups:
        state[:, slot(y, i, 4)] = jnp.concatenate([hidden[:, place(y, d)] for d in ds], axis=1)

    for step in range(2):
        total = jnp.zeros((ROWS, LANES), jnp.float32)
        for y, i, ds in groups:
            for j in range(4):
                v = state[:, slot(y, i + j, 1)].astype(jnp.float32)
                total = total + v * v
        scale = lax.rsqrt(jnp.sum(total, axis=1, keepdims=True) / WIDTH + EPS)
        scale = jnp.broadcast_to(scale, (ROWS, 4 * LANES))
        rank = jnp.zeros((ROWS, 2 * RANK), jnp.float32)
        for y, i, ds in groups:
            v = (state[:, slot(y, i, 4)].astype(jnp.float32) * scale).astype(jnp.bfloat16)
            rank = rank + lax.dot_general(
                v, panels(step, 0, y, ds), (((1,), (1,)), ((), ())),
                preferred_element_type=jnp.float32,
            )
        rank = jnp.where(own, rank, 0.0).astype(jnp.bfloat16)
        for y, i, ds in groups:
            delta = jnp.dot(rank, panels(step, 1, y, ds), preferred_element_type=jnp.float32)
            delta = delta.astype(jnp.bfloat16).astype(jnp.float32)
            new = state[:, slot(y, i, 4)].astype(jnp.float32) + ADAPTER_SCALE * delta
            new = new.astype(jnp.bfloat16)
            if step == 0:
                state[:, slot(y, i, 4)] = new
            else:
                for j, d in enumerate(ds):
                    out[:, place(y, d)] = new[:, j * LANES : (j + 1) * LANES]


def layers(z, hidden, first, second):
    whole = lambda i, z: (0, 0)
    return pl.pallas_call(
        layers_kernel,
        out_shape=jax.ShapeDtypeStruct((ROWS, WIDTH), jnp.bfloat16),
        grid_spec=pltpu.PrefetchScalarGridSpec(
            num_scalar_prefetch=1,
            grid=(1,),
            in_specs=[pl.BlockSpec((ROWS, WIDTH), whole, pipeline_mode=pl.Buffered(1))]
            + [
                pl.BlockSpec(
                    (Y, 1) + f.shape[2:], lambda i, z: (0,) * 6, pipeline_mode=pl.Buffered(1)
                )
                for f in first
            ]
            + [
                pl.BlockSpec(s.shape, lambda i, z: (0,) * 5, pipeline_mode=pl.Buffered(1))
                for s in second
            ],
            out_specs=pl.BlockSpec((ROWS, WIDTH), whole, pipeline_mode=pl.Buffered(1)),
            scratch_shapes=[pltpu.VMEM((ROWS, WIDTH), jnp.bfloat16)],
        ),
        compiler_params=pltpu.CompilerParams(vmem_limit_bytes=40 << 20),
        cost_estimate=pl.CostEstimate(
            flops=1 << 30, transcendentals=0, bytes_accessed=12 << 20
        ),
    )(z, hidden, *first, *second)


def shards(hidden, store_a, store_b, request_start, request_adapter):
    state = hidden[0]
    mine = block_adapters(request_start[0], request_adapter[0], Y * Z * ROWS)
    segments = X * CORES
    behind = lax.ppermute(mine, SEGMENT, [(s, (s + 1) % segments) for s in range(segments)])
    z = lax.axis_index("z")

    def at_z(chosen):
        rows = chosen.reshape(Y, Z, 2)
        here = lax.broadcasted_iota(jnp.int32, rows.shape, 1) == z
        return jnp.sum(jnp.where(here, rows, 0), axis=1)

    wanted = jnp.stack([at_z(mine), at_z(behind)], axis=1)

    up = [(i, (i + 1) % Z) for i in range(Z)]
    down = [(i, (i - 1) % Z) for i in range(Z)]
    chunks = {(0, 0): store_a[0], (1, 0): store_b[0]}
    for step in range(1, 9):
        for s in (0, 1):
            if step < 8 or s == 0:
                chunks[s, step] = lax.ppermute(chunks[s, step - 1], "z", up)
            if step < 8 or s == 1:
                chunks[s, Z - step] = lax.ppermute(chunks[s, (Z + 1 - step) % Z], "z", down)

    first, second = [], []
    for batch in BATCHES:
        picked = pick(wanted, [chunks[entry] for entry in batch])
        received = lax.all_to_all(picked, "y", split_axis=0, concat_axis=0, tiled=True)
        first.append(received)
        second.append(
            lax.ppermute(
                received[:, 1], SEGMENT, [(s, (s - 1) % segments) for s in range(segments)]
            )
        )
    return layers(z.astype(jnp.int32)[None], state, first, second)[None]


def solution(mesh):
    grid = Mesh(mesh.devices.reshape(X, CORES, Y, Z), ("x", "core", "y", "z"))
    return jax.shard_map(
        shards,
        mesh=grid,
        in_specs=(
            P(SEGMENT, ("y", "z"), None),
            P(SEGMENT, None, None, ("y", "z")),
            P(SEGMENT, None, None, ("y", "z")),
            P(SEGMENT, None),
            P(SEGMENT, None),
        ),
        out_specs=P(SEGMENT, ("y", "z"), None),
        check_vma=False,
    )
```

```python
import functools

import jax
import jax.numpy as jnp
from jax import lax
from jax.experimental import pallas as pl
from jax.experimental.pallas import tpu as pltpu
from jax.sharding import Mesh, PartitionSpec as P

BLOCK = 64
EPS = 1e-05
ADAPTER_SCALE = 0.5
X, CORES, Y, Z = 4, 2, 4, 16
SEGMENT = ("x", "core")
LANES = 128
ROWS = 128
WIDTH = 8192
RANK = 64

BATCHES = ((0, 1, 15), (2, 14, 3, 13), (4, 12, 5, 11), (6, 10, 7, 9), (8,))
ORDER = tuple(d for batch in BATCHES for d in batch)
PARTS = 2
PART = RANK // PARTS


def block_adapters(starts, adapters, total_rows):
    blocks = total_rows // BLOCK
    block_start = jnp.arange(blocks, dtype=jnp.int32) * BLOCK
    request = jnp.sum((starts[None, :] <= block_start[:, None]).astype(jnp.int32), axis=1) - 1
    labels = jnp.arange(adapters.shape[0], dtype=jnp.int32)
    picked = jnp.where(request[:, None] == labels[None, :], adapters[None, :], 0)
    return jnp.sum(picked, axis=1)


def pick_kernel(count, *refs):
    wanted, chunks, out, sem = refs[0], refs[1 : 1 + count], refs[-2], refs[-1]
    for y in range(Y):
        for k in range(2):
            for b in range(2):
                which = wanted[y, k, b]
                for c in range(count):
                    pltpu.make_async_copy(chunks[c].at[which], out.at[y, k, c, b], sem).start()
    pltpu.make_async_copy(out, out, sem).wait()


def pick(wanted, chunks, after):
    count = len(chunks)
    anywhere = pl.BlockSpec(memory_space=pltpu.HBM)
    return pl.pallas_call(
        functools.partial(pick_kernel, count),
        out_shape=jax.ShapeDtypeStruct((Y, 2, count, 2, RANK, LANES), jnp.bfloat16),
        in_specs=[pl.BlockSpec(memory_space=pltpu.SMEM)] + [anywhere] * (count + len(after)),
        out_specs=anywhere,
        scratch_shapes=[pltpu.SemaphoreType.DMA],
        cost_estimate=pl.CostEstimate(
            flops=0, transcendentals=0, bytes_accessed=count * (1 << 19)
        ),
    )(wanted, *chunks, *after)


def pick_gathered_kernel(wanted, gathered, *refs):
    mine, theirs, sem, their_sem = refs[-4:]
    for k, (out, s) in enumerate(((mine, sem), (theirs, their_sem))):
        for y in range(Y):
            for b in range(2):
                pltpu.make_async_copy(
                    gathered.at[:, wanted[y, k, b]], out.at[y, :, b], s
                ).start()
    pltpu.make_async_copy(mine, mine, sem).wait()
    pltpu.make_async_copy(theirs, theirs, their_sem).wait()


def pick_gathered(wanted, gathered, after):
    anywhere = pl.BlockSpec(memory_space=pltpu.HBM)
    return pl.pallas_call(
        pick_gathered_kernel,
        out_shape=[jax.ShapeDtypeStruct((Y, Z, 2, PART, LANES), jnp.bfloat16)] * 2,
        in_specs=[pl.BlockSpec(memory_space=pltpu.SMEM)] + [anywhere] * (1 + len(after)),
        out_specs=[anywhere] * 2,
        scratch_shapes=[pltpu.SemaphoreType.DMA] * 2,
        cost_estimate=pl.CostEstimate(
            flops=0, transcendentals=0, bytes_accessed=(8 << 20) // PARTS
        ),
    )(wanted, gathered, *after)


def layers_kernel(z_ref, *refs):
    n, m = len(BATCHES), PARTS
    hidden_hbm, refs = refs[0], refs[1:]
    down, refs = (refs[:m], refs[m : 2 * m]), refs[2 * m :]
    first, second, refs = refs[:n], refs[n : 2 * n], refs[2 * n :]
    out_hbm, hidden, state, out, a0, b0, a1, b1, sems = refs
    z = z_ref[0]
    copies = {}

    def copy(key, src, dst):
        copies.setdefault(key, []).append(
            pltpu.make_async_copy(src, dst, sems.at[sum(len(v) for v in copies.values())])
        )

    copy("hidden", hidden_hbm, hidden)
    for step, a_ref, b_ref in ((0, a0, b0), (1, a1, b1)):
        for p in range(PARTS):
            copy((step, 0), down[step][p], a_ref.at[:, :, :, pl.ds(p * PART, PART)])
        at = 0
        for b, batch in enumerate(BATCHES):
            src = first[b].at[:, 0] if step == 0 else second[b]
            copy((step, 1), src, b_ref.at[:, pl.ds(at, len(batch))])
            at += len(batch)
    for group in copies.values():
        for c in group:
            c.start()

    def arrived(key):
        for c in copies[key]:
            c.wait()

    def source(d):
        return (z - d) & (Z - 1)

    def place(y, d):
        return pl.ds(pl.multiple_of((y * Z + source(d)) * LANES, LANES), LANES)

    def down_panels(ref, y, ds):
        return jnp.concatenate(
            [ref[y, source(d)].reshape(2 * RANK, LANES) for d in ds], axis=1
        )

    def up_panels(ref, y, i):
        return jnp.concatenate(
            [ref[y, i + j].reshape(2 * RANK, LANES) for j in range(4)], axis=1
        )

    own = lax.broadcasted_iota(jnp.int32, (ROWS, 2 * RANK), 0) // BLOCK == (
        lax.broadcasted_iota(jnp.int32, (ROWS, 2 * RANK), 1) // RANK
    )
    groups = [(y, i, ORDER[i : i + 4]) for y in range(Y) for i in range(0, Z, 4)]

    def slot(y, i, width):
        return pl.ds((y * Z + i) * LANES, width * LANES)

    arrived("hidden")
    total = jnp.zeros((ROWS, LANES), jnp.float32)
    for y, i, ds in groups:
        for j, d in enumerate(ds):
            v = hidden[:, place(y, d)]
            state[:, slot(y, i + j, 1)] = v
            v = v.astype(jnp.float32)
            total = total + v * v

    for step, a_ref, b_ref in ((0, a0, b0), (1, a1, b1)):
        scale = lax.rsqrt(jnp.sum(total, axis=1, keepdims=True) / WIDTH + EPS)
        scale = jnp.broadcast_to(scale, (ROWS, 4 * LANES))
        rank = jnp.zeros((ROWS, 2 * RANK), jnp.float32)
        arrived((step, 0))
        for y, i, ds in groups:
            v = (state[:, slot(y, i, 4)].astype(jnp.float32) * scale).astype(jnp.bfloat16)
            rank = rank + lax.dot_general(
                v, down_panels(a_ref, y, ds), (((1,), (1,)), ((), ())),
                preferred_element_type=jnp.float32,
            )
        rank = jnp.where(own, rank, 0.0).astype(jnp.bfloat16)
        total = jnp.zeros((ROWS, LANES), jnp.float32)
        arrived((step, 1))
        for y, i, ds in groups:
            delta = jnp.dot(rank, up_panels(b_ref, y, i), preferred_element_type=jnp.float32)
            delta = delta.astype(jnp.bfloat16).astype(jnp.float32)
            new = state[:, slot(y, i, 4)].astype(jnp.float32) + ADAPTER_SCALE * delta
            new = new.astype(jnp.bfloat16)
            if step == 0:
                state[:, slot(y, i, 4)] = new
                v = new.astype(jnp.float32)
                v = v * v
                for j in range(4):
                    total = total + v[:, j * LANES : (j + 1) * LANES]
            else:
                for j, d in enumerate(ds):
                    out[:, place(y, d)] = new[:, j * LANES : (j + 1) * LANES]
                if i + 4 == Z:
                    part = pl.ds(y * Z * LANES, Z * LANES)
                    copy("out", out.at[:, part], out_hbm.at[:, part])
                    copies["out"][-1].start()
    arrived("out")


def layers(z, hidden, down, first, second):
    anywhere = pl.BlockSpec(memory_space=pltpu.HBM)
    rows = pltpu.VMEM((ROWS, WIDTH), jnp.bfloat16)
    store = pltpu.VMEM((Y, Z, 2, RANK, LANES), jnp.bfloat16)
    return pl.pallas_call(
        layers_kernel,
        out_shape=jax.ShapeDtypeStruct((ROWS, WIDTH), jnp.bfloat16),
        in_specs=[pl.BlockSpec(memory_space=pltpu.SMEM)]
        + [anywhere] * (1 + 2 * PARTS + 2 * len(BATCHES)),
        out_specs=anywhere,
        scratch_shapes=[rows] * 3
        + [store] * 4
        + [pltpu.SemaphoreType.DMA((1 + 2 * PARTS + 2 * len(BATCHES) + Y,))],
        compiler_params=pltpu.CompilerParams(vmem_limit_bytes=32 << 20),
        cost_estimate=pl.CostEstimate(
            flops=1 << 30, transcendentals=0, bytes_accessed=12 << 20
        ),
    )(z, hidden, *down[0], *down[1], *first, *second)


def after(value, *others):
    return lax.optimization_barrier((value, *others))[0]


def shards(hidden, store_a, store_b, request_start, request_adapter):
    mine = block_adapters(request_start[0], request_adapter[0], Y * Z * ROWS)
    segments = X * CORES
    ahead = [(s, (s + 1) % segments) for s in range(segments)]
    back = [(s, (s - 1) % segments) for s in range(segments)]
    behind = lax.ppermute(mine, SEGMENT, ahead)
    z = lax.axis_index("z")

    def at_z(chosen):
        rows = chosen.reshape(Y, Z, 2)
        here = lax.broadcasted_iota(jnp.int32, rows.shape, 1) == z
        return jnp.sum(jnp.where(here, rows, 0), axis=1)

    wanted = jnp.stack([at_z(mine), at_z(behind)], axis=1)

    def over_y(x):
        return lax.all_to_all(x, "y", split_axis=0, concat_axis=0, tiled=True)

    parts = [
        lax.all_gather(store_a[0][:, p * PART : (p + 1) * PART], "z") for p in range(PARTS)
    ]
    down = ([], [])

    def send_down(after):
        ours, theirs = pick_gathered(wanted, parts[len(down[0])], after)
        down[0].append(over_y(ours))
        down[1].append(over_y(lax.ppermute(theirs, SEGMENT, back)))
        return ours

    up = [(i, (i + 1) % Z) for i in range(Z)]
    low = [(i, (i - 1) % Z) for i in range(Z)]
    chunks = {0: store_b[0]}
    first, second = [], []
    for step in range(1, 9):
        if step == 6:
            chunks[5] = after(chunks[5], send_down([chunks[4]]))
        if step == 8:
            chunks[7] = after(chunks[7], down[1][0])
        chunks[step] = lax.ppermute(chunks[step - 1], "z", up)
        if step < 8:
            chunks[Z - step] = lax.ppermute(chunks[(Z + 1 - step) % Z], "z", low)
        b = len(first)
        if all(d in chunks for d in BATCHES[b]):
            picked = pick(wanted, [chunks[d] for d in BATCHES[b]], second[b - 2 : b - 1] if b > 1 else [])
            received = over_y(picked)
            first.append(received)
            second.append(lax.ppermute(received[:, 1], SEGMENT, back))
    send_down([chunks[8]])
    return layers(z.astype(jnp.int32)[None], hidden[0], down, first, second)[None]


def solution(mesh):
    grid = Mesh(mesh.devices.reshape(X, CORES, Y, Z), ("x", "core", "y", "z"))
    return jax.shard_map(
        shards,
        mesh=grid,
        in_specs=(
            P(SEGMENT, ("y", "z"), None),
            P(SEGMENT, None, None, ("y", "z")),
            P(SEGMENT, None, None, ("y", "z")),
            P(SEGMENT, None),
            P(SEGMENT, None),
        ),
        out_specs=P(SEGMENT, ("y", "z"), None),
        check_vma=False,
    )
```

```python
import functools

import jax
import jax.numpy as jnp
from jax import lax
from jax.experimental import pallas as pl
from jax.experimental.pallas import tpu as pltpu
from jax.sharding import Mesh, PartitionSpec as P

BLOCK = 64
EPS = 1e-05
ADAPTER_SCALE = 0.5
X, CORES, Y, Z = 4, 2, 4, 16
SEGMENT = ("x", "core")
LANES = 128
ROWS = 128
WIDTH = 8192
RANK = 64

BATCHES = ((0, 1, 15), (2, 14, 3, 13), (4, 12, 5, 11), (6, 10), (7, 9, 8))
ORDER = tuple(d for batch in BATCHES for d in batch)

def block_adapters(starts, adapters, total_rows):
    blocks = total_rows // BLOCK
    block_start = jnp.arange(blocks, dtype=jnp.int32) * BLOCK
    request = jnp.sum((starts[None, :] <= block_start[:, None]).astype(jnp.int32), axis=1) - 1
    labels = jnp.arange(adapters.shape[0], dtype=jnp.int32)
    picked = jnp.where(request[:, None] == labels[None, :], adapters[None, :], 0)
    return jnp.sum(picked, axis=1)


def pick_kernel(count, wanted, *refs):
    out = refs[-1]
    for y in range(Y):
        for k in range(2):
            for b in range(2):
                which = wanted[y, k, b]
                for c in range(count):
                    out[y, k, c, b] = refs[c][which]


def pick(wanted, chunks, after):
    count = len(chunks)
    return pl.pallas_call(
        functools.partial(pick_kernel, count),
        out_shape=jax.ShapeDtypeStruct((Y, 2, count, 2, RANK, LANES), jnp.bfloat16),
        in_specs=[pl.BlockSpec(memory_space=pltpu.SMEM)]
        + [pl.BlockSpec(memory_space=pltpu.VMEM)] * count
        + [pl.BlockSpec(memory_space=pl.ANY)] * len(after),
        out_specs=pl.BlockSpec(memory_space=pltpu.VMEM),
        compiler_params=pltpu.CompilerParams(vmem_limit_bytes=12 << 20),
        cost_estimate=pl.CostEstimate(
            flops=0, transcendentals=0, bytes_accessed=count * (3 << 18)
        ),
    )(wanted, *chunks, *after)


def norm_kernel(hidden, out):
    total = jnp.zeros((ROWS, LANES), jnp.float32)
    for i in range(WIDTH // LANES):
        v = hidden[:, i * LANES : (i + 1) * LANES].astype(jnp.float32)
        total = total + v * v
    scale = lax.rsqrt(jnp.sum(total, axis=1, keepdims=True) / WIDTH + EPS)
    scale = jnp.broadcast_to(scale, (ROWS, LANES))
    for y in range(Y):
        for i in range(Z):
            v = hidden[:, (y * Z + i) * LANES : (y * Z + i + 1) * LANES].astype(jnp.float32)
            out[y, :, i * LANES : (i + 1) * LANES] = (v * scale).astype(jnp.bfloat16)


def norm(hidden):
    vmem = pl.BlockSpec(memory_space=pltpu.VMEM)
    return pl.pallas_call(
        norm_kernel,
        out_shape=jax.ShapeDtypeStruct((Y, ROWS, Z * LANES), jnp.bfloat16),
        in_specs=[vmem],
        out_specs=vmem,
        compiler_params=pltpu.CompilerParams(vmem_limit_bytes=12 << 20),
        cost_estimate=pl.CostEstimate(
            flops=1 << 22, transcendentals=0, bytes_accessed=4 << 20
        ),
    )(hidden)


HALF = RANK // 2


def down_kernel(wanted, gathered, normed, *refs):
    *halves, partial = refs[-3:]
    for y in range(Y):
        for b in range(2):
            which = wanted[y, 1, b]
            for z in range(Z):
                for h, theirs in enumerate(halves):
                    theirs[y, z, b] = gathered[z, which, h * HALF : (h + 1) * HALF]
    for y in range(Y):
        for b in range(2):
            which = wanted[y, 0, b]
            rows = slice(b * BLOCK, (b + 1) * BLOCK)
            panel = jnp.concatenate([gathered[z, which] for z in range(Z)], axis=1)
            product = lax.dot_general(
                normed[y, rows], panel, (((1,), (1,)), ((), ())),
                preferred_element_type=jnp.float32,
            )
            partial[y, rows] = jnp.concatenate([product, product], axis=1)


def down(wanted, gathered, normed, *after):
    vmem = pl.BlockSpec(memory_space=pltpu.VMEM)
    return pl.pallas_call(
        down_kernel,
        out_shape=[
            jax.ShapeDtypeStruct((Y, Z, 2, HALF, LANES), jnp.bfloat16),
            jax.ShapeDtypeStruct((Y, Z, 2, HALF, LANES), jnp.bfloat16),
            jax.ShapeDtypeStruct((Y, ROWS, 2 * RANK), jnp.float32),
        ],
        in_specs=[pl.BlockSpec(memory_space=pltpu.SMEM), vmem, vmem]
        + [pl.BlockSpec(memory_space=pl.ANY)] * len(after),
        out_specs=[vmem] * 3,
        compiler_params=pltpu.CompilerParams(vmem_limit_bytes=20 << 20),
        cost_estimate=pl.CostEstimate(
            flops=1 << 27, transcendentals=0, bytes_accessed=12 << 20
        ),
    )(wanted, gathered, normed, *after)


def place(z, y, d):
    return pl.ds(pl.multiple_of((y * Z + ((z - d) & (Z - 1))) * LANES, LANES), LANES)


def slot(y, i, width):
    return pl.ds((y * Z + i) * LANES, width * LANES)


def up_panels(ref, y, i):
    return jnp.concatenate(
        [ref[y, i + j].reshape(2 * RANK, LANES) for j in range(4)], axis=1
    )


def own_block():
    return lax.broadcasted_iota(jnp.int32, (ROWS, 2 * RANK), 0) // BLOCK == (
        lax.broadcasted_iota(jnp.int32, (ROWS, 2 * RANK), 1) // RANK
    )


GROUPS = tuple((y, i, ORDER[i : i + 4]) for y in range(Y) for i in range(0, Z, 4))


def updated(state, rank, panel):
    delta = jnp.dot(rank, panel, preferred_element_type=jnp.float32)
    delta = delta.astype(jnp.bfloat16).astype(jnp.float32)
    return (state.astype(jnp.float32) + ADAPTER_SCALE * delta).astype(jnp.bfloat16)


def first_kernel(z_ref, rank_ref, hidden_hbm, *refs):
    n = len(BATCHES)
    batches, state_hbm = refs[:n], refs[n]
    hidden, state, panels, sems = refs[n + 1 :]
    z = z_ref[0]
    loads = [pltpu.make_async_copy(hidden_hbm, hidden, sems.at[0])]
    at = 0
    for b, batch in enumerate(BATCHES):
        loads.append(
            pltpu.make_async_copy(
                batches[b].at[:, 0], panels.at[:, pl.ds(at, len(batch))], sems.at[b + 1]
            )
        )
        at += len(batch)
    for c in loads:
        c.start()
    rank = rank_ref[0]
    for y in range(1, Y):
        rank = rank + rank_ref[y]
    rank = jnp.where(own_block(), rank, 0.0).astype(jnp.bfloat16)
    for c in loads:
        c.wait()
    stores = []
    for y, i, ds in GROUPS:
        old = jnp.concatenate([hidden[:, place(z, y, d)] for d in ds], axis=1)
        state[:, slot(y, i, 4)] = updated(old, rank, up_panels(panels, y, i))
        if i + 4 == Z:
            part = slot(y, 0, Z)
            stores.append(
                pltpu.make_async_copy(
                    state.at[:, part], state_hbm.at[:, part], sems.at[n + 1 + y]
                )
            )
            stores[-1].start()
    for c in stores:
        c.wait()


def second_kernel(z_ref, state_hbm, *refs):
    halves, refs = refs[:2], refs[2:]
    n = len(BATCHES)
    batches, out_hbm = refs[:n], refs[n]
    state, low, panels, out, sems = refs[n + 1 :]
    z = z_ref[0]
    state_in = pltpu.make_async_copy(state_hbm, state, sems.at[0])
    low_in = [
        pltpu.make_async_copy(
            half, low.at[:, :, :, pl.ds(h * HALF, HALF)], sems.at[n + 2 + Y + h]
        )
        for h, half in enumerate(halves)
    ]
    loads = []
    at = 0
    for b, batch in enumerate(BATCHES):
        loads.append(
            pltpu.make_async_copy(
                batches[b], panels.at[:, pl.ds(at, len(batch))], sems.at[b + 2]
            )
        )
        at += len(batch)
    for c in [state_in] + low_in + loads:
        c.start()
    state_in.wait()
    total = jnp.zeros((ROWS, LANES), jnp.float32)
    for y, i, ds in GROUPS:
        for j in range(4):
            v = state[:, slot(y, i + j, 1)].astype(jnp.float32)
            total = total + v * v
    scale = lax.rsqrt(jnp.sum(total, axis=1, keepdims=True) / WIDTH + EPS)
    scale = jnp.broadcast_to(scale, (ROWS, 4 * LANES))
    rank = jnp.zeros((ROWS, 2 * RANK), jnp.float32)
    for c in low_in:
        c.wait()
    for y, i, ds in GROUPS:
        v = (state[:, slot(y, i, 4)].astype(jnp.float32) * scale).astype(jnp.bfloat16)
        panel = jnp.concatenate(
            [low[y, (z - d) & (Z - 1)].reshape(2 * RANK, LANES) for d in ds], axis=1
        )
        rank = rank + lax.dot_general(
            v, panel, (((1,), (1,)), ((), ())), preferred_element_type=jnp.float32
        )
    rank = jnp.where(own_block(), rank, 0.0).astype(jnp.bfloat16)
    for c in loads:
        c.wait()
    stores = []
    for y, i, ds in GROUPS:
        new = updated(state[:, slot(y, i, 4)], rank, up_panels(panels, y, i))
        for j, d in enumerate(ds):
            out[:, place(z, y, d)] = new[:, j * LANES : (j + 1) * LANES]
        if i + 4 == Z:
            part = slot(y, 0, Z)
            stores.append(
                pltpu.make_async_copy(
                    out.at[:, part], out_hbm.at[:, part], sems.at[n + 2 + y]
                )
            )
            stores[-1].start()
    for c in stores:
        c.wait()


ROW_BUFFER = pltpu.VMEM((ROWS, WIDTH), jnp.bfloat16)
PANEL_BUFFER = pltpu.VMEM((Y, Z, 2, RANK, LANES), jnp.bfloat16)


def layer_call(kernel, in_specs, scratch, *operands):
    anywhere = pl.BlockSpec(memory_space=pl.ANY)
    return pl.pallas_call(
        kernel,
        out_shape=jax.ShapeDtypeStruct((ROWS, WIDTH), jnp.bfloat16),
        in_specs=in_specs + [anywhere] * (len(operands) - len(in_specs)),
        out_specs=anywhere,
        scratch_shapes=scratch + [pltpu.SemaphoreType.DMA((4 + len(BATCHES) + Y,))],
        compiler_params=pltpu.CompilerParams(vmem_limit_bytes=60 << 20),
        cost_estimate=pl.CostEstimate(
            flops=1 << 29, transcendentals=0, bytes_accessed=6 << 20
        ),
    )(*operands)


def after(value, *others):
    return lax.optimization_barrier((value, *others))[0]


def shards(hidden, store_a, store_b, request_start, request_adapter):
    mine = block_adapters(request_start[0], request_adapter[0], Y * Z * ROWS)
    segments = X * CORES
    ahead = [(s, (s + 1) % segments) for s in range(segments)]
    back = [(s, (s - 1) % segments) for s in range(segments)]
    behind = lax.ppermute(mine, SEGMENT, ahead)
    z = lax.axis_index("z")

    def at_z(chosen):
        rows = chosen.reshape(Y, Z, 2)
        here = lax.broadcasted_iota(jnp.int32, rows.shape, 1) == z
        return jnp.sum(jnp.where(here, rows, 0), axis=1)

    wanted = jnp.stack([at_z(mine), at_z(behind)], axis=1)

    def over_y(x):
        return lax.all_to_all(x, "y", split_axis=0, concat_axis=0, tiled=True)

    gathered = lax.all_gather(store_a[0], "z")
    normed = over_y(norm(hidden[0]))

    up = [(i, (i + 1) % Z) for i in range(Z)]
    low = [(i, (i - 1) % Z) for i in range(Z)]
    chunks = {0: store_b[0]}
    first, second = [], []

    def send_on(*earlier):
        picked = pick(wanted, [chunks[d] for d in BATCHES[len(first)]], earlier)
        received = over_y(picked)
        first.append(received)
        second.append(lax.ppermute(received[:, 1], SEGMENT, back))
        return picked

    for step in range(1, 9):
        chunks[step] = lax.ppermute(chunks[step - 1], "z", up)
        if step < 8:
            chunks[Z - step] = lax.ppermute(chunks[(Z + 1 - step) % Z], "z", low)
        b = len(first)
        if b < 4 and all(d in chunks for d in BATCHES[b]):
            picked = send_on(*second[b - 2 : b - 1] if b > 1 else (normed,) if b == 0 else ())
    *halves, partial = down(wanted, gathered, normed, chunks[6])
    halves = [lax.ppermute(half, SEGMENT, back) for half in halves]
    rank = over_y(after(partial, chunks[7], chunks[9]))
    halves = [over_y(after(halves[0], rank)), over_y(after(halves[1], chunks[8]))]
    send_on(second[2], rank)
    z = z.astype(jnp.int32)[None]
    smem, vmem = (pl.BlockSpec(memory_space=m) for m in (pltpu.SMEM, pltpu.VMEM))
    state = layer_call(
        first_kernel, [smem, vmem], [ROW_BUFFER] * 2 + [PANEL_BUFFER], z, rank, hidden[0], *first
    )
    updated_rows = layer_call(
        second_kernel, [smem], [ROW_BUFFER] + [PANEL_BUFFER] * 2 + [ROW_BUFFER],
        z, state, *halves, *second,
    )
    return updated_rows[None]


def solution(mesh):
    grid = Mesh(mesh.devices.reshape(X, CORES, Y, Z), ("x", "core", "y", "z"))
    return jax.shard_map(
        shards,
        mesh=grid,
        in_specs=(
            P(SEGMENT, ("y", "z"), None),
            P(SEGMENT, None, None, ("y", "z")),
            P(SEGMENT, None, None, ("y", "z")),
            P(SEGMENT, None),
            P(SEGMENT, None),
        ),
        out_specs=P(SEGMENT, ("y", "z"), None),
        check_vma=False,
    )
```

```python
import functools

import jax
import jax.numpy as jnp
from jax import lax
from jax.experimental import pallas as pl
from jax.experimental.pallas import tpu as pltpu
from jax.sharding import Mesh, PartitionSpec as P

BLOCK = 64
EPS = 1e-05
ADAPTER_SCALE = 0.5
X, CORES, Y, Z = 4, 2, 4, 16
SEGMENT = ("x", "core")
LANES = 128
ROWS = 128
WIDTH = 8192
RANK = 64

BATCHES = ((0, 1, 15), (2, 14, 3, 13), (4, 12, 5, 11), (6, 10), (7, 9, 8))
ORDER = tuple(d for batch in BATCHES for d in batch)

def block_adapters(starts, adapters, total_rows):
    blocks = total_rows // BLOCK
    block_start = jnp.arange(blocks, dtype=jnp.int32) * BLOCK
    request = jnp.sum((starts[None, :] <= block_start[:, None]).astype(jnp.int32), axis=1) - 1
    labels = jnp.arange(adapters.shape[0], dtype=jnp.int32)
    picked = jnp.where(request[:, None] == labels[None, :], adapters[None, :], 0)
    return jnp.sum(picked, axis=1)


def pick_kernel(count, wanted, *refs):
    out = refs[-1]
    for y in range(Y):
        for k in range(2):
            for b in range(2):
                which = wanted[y, k, b]
                for c in range(count):
                    out[y, k, c, b] = refs[c][which]


def pick(wanted, chunks, after):
    count = len(chunks)
    return pl.pallas_call(
        functools.partial(pick_kernel, count),
        out_shape=jax.ShapeDtypeStruct((Y, 2, count, 2, RANK, LANES), jnp.bfloat16),
        in_specs=[pl.BlockSpec(memory_space=pltpu.SMEM)]
        + [pl.BlockSpec(memory_space=pltpu.VMEM)] * count
        + [pl.BlockSpec(memory_space=pl.ANY)] * len(after),
        out_specs=pl.BlockSpec(memory_space=pltpu.VMEM),
        compiler_params=pltpu.CompilerParams(vmem_limit_bytes=12 << 20),
        cost_estimate=pl.CostEstimate(
            flops=0, transcendentals=0, bytes_accessed=count * (3 << 18)
        ),
    )(wanted, *chunks, *after)


def norm_kernel(hidden, out):
    total = jnp.zeros((ROWS, LANES), jnp.float32)
    for i in range(WIDTH // LANES):
        v = hidden[:, i * LANES : (i + 1) * LANES].astype(jnp.float32)
        total = total + v * v
    scale = lax.rsqrt(jnp.sum(total, axis=1, keepdims=True) / WIDTH + EPS)
    scale = jnp.broadcast_to(scale, (ROWS, LANES))
    for y in range(Y):
        for i in range(Z):
            v = hidden[:, (y * Z + i) * LANES : (y * Z + i + 1) * LANES].astype(jnp.float32)
            out[y, :, i * LANES : (i + 1) * LANES] = (v * scale).astype(jnp.bfloat16)


def norm(hidden):
    vmem = pl.BlockSpec(memory_space=pltpu.VMEM)
    return pl.pallas_call(
        norm_kernel,
        out_shape=jax.ShapeDtypeStruct((Y, ROWS, Z * LANES), jnp.bfloat16),
        in_specs=[vmem],
        out_specs=vmem,
        compiler_params=pltpu.CompilerParams(vmem_limit_bytes=12 << 20),
        cost_estimate=pl.CostEstimate(
            flops=1 << 22, transcendentals=0, bytes_accessed=4 << 20
        ),
    )(hidden)


HALF = RANK // 2


def down_kernel(wanted, gathered, normed, *refs):
    *halves, partial = refs[-3:]
    for y in range(Y):
        for b in range(2):
            which = wanted[y, 1, b]
            for z in range(Z):
                for h, theirs in enumerate(halves):
                    theirs[y, z, b] = gathered[z, which, h * HALF : (h + 1) * HALF]
    for y in range(Y):
        for b in range(2):
            which = wanted[y, 0, b]
            rows = slice(b * BLOCK, (b + 1) * BLOCK)
            panel = jnp.concatenate([gathered[z, which] for z in range(Z)], axis=1)
            product = lax.dot_general(
                normed[y, rows], panel, (((1,), (1,)), ((), ())),
                preferred_element_type=jnp.float32,
            )
            partial[y, rows] = jnp.concatenate([product, product], axis=1)


def down(wanted, gathered, normed, *after):
    vmem = pl.BlockSpec(memory_space=pltpu.VMEM)
    return pl.pallas_call(
        down_kernel,
        out_shape=[
            jax.ShapeDtypeStruct((Y, Z, 2, HALF, LANES), jnp.bfloat16),
            jax.ShapeDtypeStruct((Y, Z, 2, HALF, LANES), jnp.bfloat16),
            jax.ShapeDtypeStruct((Y, ROWS, 2 * RANK), jnp.float32),
        ],
        in_specs=[pl.BlockSpec(memory_space=pltpu.SMEM), vmem, vmem]
        + [pl.BlockSpec(memory_space=pl.ANY)] * len(after),
        out_specs=[vmem] * 3,
        compiler_params=pltpu.CompilerParams(vmem_limit_bytes=20 << 20),
        cost_estimate=pl.CostEstimate(
            flops=1 << 27, transcendentals=0, bytes_accessed=12 << 20
        ),
    )(wanted, gathered, normed, *after)


def place(z, y, d):
    return pl.ds(pl.multiple_of((y * Z + ((z - d) & (Z - 1))) * LANES, LANES), LANES)


def slot(y, i, width):
    return pl.ds((y * Z + i) * LANES, width * LANES)


def up_panels(ref, y, i):
    return jnp.concatenate(
        [ref[y, i + j].reshape(2 * RANK, LANES) for j in range(4)], axis=1
    )


def own_block():
    return lax.broadcasted_iota(jnp.int32, (ROWS, 2 * RANK), 0) // BLOCK == (
        lax.broadcasted_iota(jnp.int32, (ROWS, 2 * RANK), 1) // RANK
    )


GROUPS = tuple((y, i, ORDER[i : i + 4]) for y in range(Y) for i in range(0, Z, 4))


def updated(state, rank, panel):
    delta = jnp.dot(rank, panel, preferred_element_type=jnp.float32)
    delta = delta.astype(jnp.bfloat16).astype(jnp.float32)
    return (state.astype(jnp.float32) + ADAPTER_SCALE * delta).astype(jnp.bfloat16)


def first_kernel(z_ref, rank_ref, hidden_hbm, *refs):
    n = len(BATCHES)
    batches, state_hbm = refs[:n], refs[n]
    hidden, state, panels, sems = refs[n + 1 :]
    z = z_ref[0]
    loads = [pltpu.make_async_copy(hidden_hbm, hidden, sems.at[0])]
    at = 0
    for b, batch in enumerate(BATCHES):
        loads.append(
            pltpu.make_async_copy(
                batches[b].at[:, 0], panels.at[:, pl.ds(at, len(batch))], sems.at[b + 1]
            )
        )
        at += len(batch)
    for c in loads:
        c.start()
    rank = rank_ref[0]
    for y in range(1, Y):
        rank = rank + rank_ref[y]
    rank = jnp.where(own_block(), rank, 0.0).astype(jnp.bfloat16)
    for c in loads:
        c.wait()
    stores = []
    for y, i, ds in GROUPS:
        old = jnp.concatenate([hidden[:, place(z, y, d)] for d in ds], axis=1)
        state[:, slot(y, i, 4)] = updated(old, rank, up_panels(panels, y, i))
        if i + 4 == Z:
            part = slot(y, 0, Z)
            stores.append(
                pltpu.make_async_copy(
                    state.at[:, part], state_hbm.at[:, part], sems.at[n + 1 + y]
                )
            )
            stores[-1].start()
    for c in stores:
        c.wait()


def second_kernel(z_ref, state_hbm, *refs):
    halves, refs = refs[:2], refs[2:]
    n = len(BATCHES)
    batches, out_hbm = refs[:n], refs[n]
    state, low, panels, out, sems = refs[n + 1 :]
    z = z_ref[0]
    state_in = pltpu.make_async_copy(state_hbm, state, sems.at[0])
    low_in = [
        pltpu.make_async_copy(
            half, low.at[:, :, :, pl.ds(h * HALF, HALF)], sems.at[n + 2 + Y + h]
        )
        for h, half in enumerate(halves)
    ]
    loads = []
    at = 0
    for b, batch in enumerate(BATCHES):
        loads.append(
            pltpu.make_async_copy(
                batches[b], panels.at[:, pl.ds(at, len(batch))], sems.at[b + 2]
            )
        )
        at += len(batch)
    for c in [state_in] + low_in + loads:
        c.start()
    state_in.wait()
    total = jnp.zeros((ROWS, LANES), jnp.float32)
    for y, i, ds in GROUPS:
        for j in range(4):
            v = state[:, slot(y, i + j, 1)].astype(jnp.float32)
            total = total + v * v
    scale = lax.rsqrt(jnp.sum(total, axis=1, keepdims=True) / WIDTH + EPS)
    scale = jnp.broadcast_to(scale, (ROWS, 4 * LANES))
    rank = jnp.zeros((ROWS, 2 * RANK), jnp.float32)
    for c in low_in:
        c.wait()
    for y, i, ds in GROUPS:
        v = (state[:, slot(y, i, 4)].astype(jnp.float32) * scale).astype(jnp.bfloat16)
        panel = jnp.concatenate(
            [low[y, (z - d) & (Z - 1)].reshape(2 * RANK, LANES) for d in ds], axis=1
        )
        rank = rank + lax.dot_general(
            v, panel, (((1,), (1,)), ((), ())), preferred_element_type=jnp.float32
        )
    rank = jnp.where(own_block(), rank, 0.0).astype(jnp.bfloat16)
    for c in loads:
        c.wait()
    stores = []
    for y, i, ds in GROUPS:
        new = updated(state[:, slot(y, i, 4)], rank, up_panels(panels, y, i))
        for j, d in enumerate(ds):
            out[:, place(z, y, d)] = new[:, j * LANES : (j + 1) * LANES]
        if i + 4 == Z:
            part = slot(y, 0, Z)
            stores.append(
                pltpu.make_async_copy(
                    out.at[:, part], out_hbm.at[:, part], sems.at[n + 2 + y]
                )
            )
            stores[-1].start()
    for c in stores:
        c.wait()


ROW_BUFFER = pltpu.VMEM((ROWS, WIDTH), jnp.bfloat16)
PANEL_BUFFER = pltpu.VMEM((Y, Z, 2, RANK, LANES), jnp.bfloat16)


def layer_call(kernel, in_specs, scratch, *operands):
    anywhere = pl.BlockSpec(memory_space=pl.ANY)
    return pl.pallas_call(
        kernel,
        out_shape=jax.ShapeDtypeStruct((ROWS, WIDTH), jnp.bfloat16),
        in_specs=in_specs + [anywhere] * (len(operands) - len(in_specs)),
        out_specs=anywhere,
        scratch_shapes=scratch + [pltpu.SemaphoreType.DMA((4 + len(BATCHES) + Y,))],
        compiler_params=pltpu.CompilerParams(vmem_limit_bytes=60 << 20),
        cost_estimate=pl.CostEstimate(
            flops=1 << 29, transcendentals=0, bytes_accessed=6 << 20
        ),
    )(*operands)


def after(value, *others):
    return lax.optimization_barrier((value, *others))[0]


def shards(hidden, store_a, store_b, request_start, request_adapter):
    mine = block_adapters(request_start[0], request_adapter[0], Y * Z * ROWS)
    segments = X * CORES
    ahead = [(s, (s + 1) % segments) for s in range(segments)]
    back = [(s, (s - 1) % segments) for s in range(segments)]
    behind = lax.ppermute(mine, SEGMENT, ahead)
    z = lax.axis_index("z")

    def at_z(chosen):
        rows = chosen.reshape(Y, Z, 2)
        here = lax.broadcasted_iota(jnp.int32, rows.shape, 1) == z
        return jnp.sum(jnp.where(here, rows, 0), axis=1)

    wanted = jnp.stack([at_z(mine), at_z(behind)], axis=1)

    def over_y(x):
        return lax.all_to_all(x, "y", split_axis=0, concat_axis=0, tiled=True)

    gathered = lax.all_gather(store_a[0], "z")
    normed = over_y(norm(hidden[0]))

    up = [(i, (i + 1) % Z) for i in range(Z)]
    low = [(i, (i - 1) % Z) for i in range(Z)]
    chunks = {0: store_b[0]}
    first, second = [], []

    def send_on(*earlier):
        picked = pick(wanted, [chunks[d] for d in BATCHES[len(first)]], earlier)
        received = over_y(picked)
        first.append(received)
        second.append(lax.ppermute(received[:, 1], SEGMENT, back))
        return picked

    for step in range(1, 9):
        chunks[step] = lax.ppermute(chunks[step - 1], "z", up)
        if step < 8:
            chunks[Z - step] = lax.ppermute(chunks[(Z + 1 - step) % Z], "z", low)
        b = len(first)
        if b < 4 and all(d in chunks for d in BATCHES[b]):
            picked = send_on(*second[b - 2 : b - 1] if b > 1 else (normed,) if b == 0 else ())
    *halves, partial = down(wanted, gathered, normed, chunks[6])
    halves = [lax.ppermute(half, SEGMENT, back) for half in halves]
    rank = over_y(after(partial, chunks[7], chunks[9]))
    halves = [over_y(after(halves[0], rank)), over_y(after(halves[1], chunks[8]))]
    send_on(second[2])
    z = z.astype(jnp.int32)[None]
    smem, vmem = (pl.BlockSpec(memory_space=m) for m in (pltpu.SMEM, pltpu.VMEM))
    state = layer_call(
        first_kernel, [smem, vmem], [ROW_BUFFER] * 2 + [PANEL_BUFFER], z, rank, hidden[0], *first
    )
    updated_rows = layer_call(
        second_kernel, [smem], [ROW_BUFFER] + [PANEL_BUFFER] * 2 + [ROW_BUFFER],
        z, state, *halves, *second,
    )
    return updated_rows[None]


def solution(mesh):
    grid = Mesh(mesh.devices.reshape(X, CORES, Y, Z), ("x", "core", "y", "z"))
    return jax.shard_map(
        shards,
        mesh=grid,
        in_specs=(
            P(SEGMENT, ("y", "z"), None),
            P(SEGMENT, None, None, ("y", "z")),
            P(SEGMENT, None, None, ("y", "z")),
            P(SEGMENT, None),
            P(SEGMENT, None),
        ),
        out_specs=P(SEGMENT, ("y", "z"), None),
        check_vma=False,
    )
```
